512 devices in a mesh: space: 64 (over z, x_lo, core), tm: 8 (over x_hi, y).
Axes of the slice: x: 4 (x_hi: 2, x_lo: 2; x = x_hi * 2 + x_lo), y: 4, z: 16, core: 2. Of those that a mesh axis runs over, the one named last changes fastest.
Arguments:
- snapshots: bfloat16 [131072, 8192], P('space', 'tm'), may hold values from -30 to 30
- omega: int32 [32, 8192], P(None, 'tm'), may hold values from -1 to 1, as said below
Outputs:
- sketch: bfloat16 [32, 131072], P(None, 'space')
- coefficients: float32 [32, 8192], P(None, 'tm')
The draws below stay inside these ranges and needn't reach their ends.
Inputs may be any that keep to these rules, and one draw needn't show every extreme that they name: `omega`: every entry is -1 or 1.
All inputs are finite; a program needn't handle non-finite values.
Results may differ from the reference program's by a relative error of at most 0.0028.
Values may be sent and summed in bfloat16 or wider, within the bound.
A program may use at most 64 MiB of HBM per device.

```python
import jax
import jax.numpy as jnp
from jax import lax

SKETCH = 32
SNAP = 8192
ROWS = 131072


def draw_snapshots(key, part):
    key_base = jax.random.fold_in(key, 11)
    key_rough = jax.random.fold_in(key, 12)
    rows_pos = jnp.arange(ROWS, dtype=jnp.float32) / ROWS
    rough = jnp.exp(jax.random.uniform(key_rough, (ROWS,), jnp.float32, 0.0, jnp.log(10.0)))
    row_scale = 0.25 * rough * jnp.exp(jnp.log(3.0) * rows_pos)
    base = jnp.clip(jax.random.normal(key_base, (ROWS, SNAP), jnp.float32), -4.0, 4.0)
    return (base * row_scale[:, None]).astype(jnp.bfloat16)


def draw_omega(key, part):
    return 2 * jax.random.randint(jax.random.fold_in(key, 21), (SKETCH, SNAP), 0, 2, jnp.int32) - 1


def setup_inputs(seed: int = 0) -> dict:
    streams_of = jax.random.split(jax.random.key(seed), 3)
    snapshots = draw_snapshots(jax.random.fold_in(streams_of[2], 71), 0)
    omega = draw_omega(jax.random.fold_in(streams_of[2], 71), 0)
    return {"snapshots": snapshots, "omega": omega}


def reference(snapshots, omega):
    signs = omega.astype(jnp.bfloat16)
    total = lax.dot_general(signs.astype(jnp.float32), snapshots.astype(jnp.float32), (((1,), (1,)), ((), ())), preferred_element_type=jnp.float32)
    sketch = (total * SNAP ** (-0.5)).astype(jnp.bfloat16)
    gram = lax.dot_general(sketch.astype(jnp.float32), sketch.astype(jnp.float32), (((1,), (1,)), ((), ())), preferred_element_type=jnp.float32)
    lower = jnp.linalg.cholesky(gram)
    projection = jnp.dot(sketch.astype(jnp.float32), snapshots.astype(jnp.float32), preferred_element_type=jnp.float32)
    coefficients = jax.scipy.linalg.solve_triangular(lower, projection, lower=True)
    return (sketch, coefficients)
```

```python
import jax
import jax.numpy as jnp
from jax import lax
from jax.experimental import pallas as pl
from jax.experimental.pallas import tpu as pltpu
from jax.sharding import PartitionSpec as P

MESH = pl.DeviceIdType.MESH
SNAP = 8192
K = 32
TM_FAR = ((1, 2), (1, 1), (1, 3), (1, 0), (0, 2), (0, 1), (0, 3))
OCT_FAR = ((1, 1, 0), (1, 1, 1), (1, 0, 0), (1, 0, 1), (0, 1, 0), (0, 1, 1), (0, 0, 1))
Z_FAR = (4, 3, 5, 2, 6, 1, 7)


def flip(bit, f):
    return (bit + f) % 2


def kernel(
    snap, omega, sketch_out, coef_out,
    a, om, part, rs, sk, pp, r8, zb, cb, g8, gz,
    in_sem, om_sem, out_sem,
    rs_send, rs_recv, ag_send, ag_recv, p8_send, p8_recv, z_send, z_recv,
    c8_send, c8_recv, g8_send, g8_recv, gz_send, gz_recv,
):
    s, t = lax.axis_index("space"), lax.axis_index("tm")
    z, xl, c = s // 4, (s // 2) % 2, s % 2
    xh, y = t // 4, t % 4
    zh, zp = z // 2, z % 2
    m = zp * 4 + xl * 2 + c
    rows = a.shape[1]

    def tm_of(off):
        return flip(xh, off[0]) * 4 + (y + off[1]) % 4

    def oct_of(f):
        q = flip(zp, f[0]) * 4 + flip(xl, f[1]) * 2 + flip(c, f[2])
        return q, (zh * 8 + q, t)

    def z_of(j):
        w = (zh + j) % 8
        return w, (w * 8 + m, t)

    om_copy = pltpu.make_async_copy(omega, om, om_sem)
    om_copy.start()
    order = [tm_of(off) for off in TM_FAR] + [t]
    loads = []
    for i, d in enumerate(order):
        cp = pltpu.make_async_copy(
            snap.at[pl.ds(pl.multiple_of(d * rows, rows), rows), :], a.at[d], in_sem.at[i]
        )
        cp.start()
        loads.append(cp)

    barrier = pltpu.get_barrier_semaphore()
    peers = [(s, tm_of(off)) for off in TM_FAR]
    peers += [oct_of(f)[1] for f in OCT_FAR] + [z_of(j)[1] for j in Z_FAR]
    for peer in peers:
        pl.semaphore_signal(barrier, inc=1, device_id=peer, device_id_type=MESH)

    def send(src, dst, send_sem, recv_sem, peer):
        return pltpu.make_async_remote_copy(
            src_ref=src, dst_ref=dst, send_sem=send_sem, recv_sem=recv_sem,
            device_id=peer, device_id_type=MESH,
        )

    om_copy.wait()
    signs = om[...].astype(jnp.float32).astype(jnp.bfloat16)
    for i, d in enumerate(order):
        loads[i].wait()
        part[i] = lax.dot_general(
            signs, a[d], (((1,), (1,)), ((), ())), preferred_element_type=jnp.float32
        )
    pl.semaphore_wait(barrier, len(peers))
    sent = []
    rs_copies = []
    for i, off in enumerate(TM_FAR):
        cp = send(part.at[i], rs.at[i], rs_send.at[i], rs_recv.at[i], (s, order[i]))
        cp.start()
        rs_copies.append(cp)
    sent += rs_copies

    total = part[7]
    for i in (5, 6, 4, 3, 1, 2, 0):
        rs_copies[i].wait_recv()
        total = total + rs[i]
    factor = SNAP ** (-0.5)
    sk[t] = (total * factor).astype(jnp.bfloat16)
    for i, off in enumerate(TM_FAR):
        cp = send(sk.at[t], sk.at[t], ag_send.at[i], ag_recv.at[t], (s, order[i]))
        cp.start()
        sent.append(cp)

    proj = None
    gram = None
    outs = []
    for i in (7, 5, 6, 4, 3, 1, 2, 0):
        d = order[i]
        if i < 7:
            send(sk.at[d], sk.at[d], ag_send.at[i], ag_recv.at[d], (s, d)).wait_recv()
        cp = pltpu.make_async_copy(
            sk.at[d], sketch_out.at[:, pl.ds(pl.multiple_of(d * rows, rows), rows)], out_sem.at[i]
        )
        cp.start()
        outs.append(cp)
        block = sk[d]
        wide = jnp.concatenate([block] * 4, axis=0)
        g = lax.dot_general(
            block, wide, (((1,), (1,)), ((), ())), preferred_element_type=jnp.float32
        )
        p = jnp.dot(block, a[d], preferred_element_type=jnp.float32)
        gram = g if gram is None else gram + g
        proj = p if proj is None else proj + p

    lane8 = lax.broadcasted_iota(jnp.int32, (8, 128), 1) // K
    packed = jnp.zeros((8, 128), jnp.float32)
    for b in range(4):
        packed = jnp.where(lane8 == b, gram[8 * b : 8 * b + 8], packed)
    g8[m] = packed
    for i, f in enumerate(OCT_FAR):
        q, peer = oct_of(f)
        cp = send(g8.at[m], g8.at[m], g8_send.at[i], g8_recv.at[m], peer)
        cp.start()
        sent.append(cp)
    for q in range(8):
        pp[q] = proj[:, 128 * q : 128 * q + 128]
    r8[m] = pp[m]
    for i, f in enumerate(OCT_FAR):
        q, peer = oct_of(f)
        cp = send(pp.at[q], r8.at[m], p8_send.at[i], p8_recv.at[m], peer)
        cp.start()
        sent.append(cp)

    for i, f in enumerate(OCT_FAR):
        q, peer = oct_of(f)
        send(g8.at[q], g8.at[q], g8_send.at[i], g8_recv.at[q], peer).wait_recv()
    gsum = g8[0]
    for q in range(1, 8):
        gsum = gsum + g8[q]
    gz[zh] = gsum
    for i, j in enumerate(Z_FAR):
        w, peer = z_of(j)
        cp = send(gz.at[zh], gz.at[zh], gz_send.at[i], gz_recv.at[zh], peer)
        cp.start()
        sent.append(cp)

    for i, f in enumerate(OCT_FAR):
        q, peer = oct_of(f)
        send(pp.at[q], r8.at[q], p8_send.at[i], p8_recv.at[q], peer).wait_recv()
    psum = r8[0]
    for q in range(1, 8):
        psum = psum + r8[q]
    zb[zh] = psum
    for i, j in enumerate(Z_FAR):
        w, peer = z_of(j)
        cp = send(zb.at[zh], zb.at[zh], z_send.at[i], z_recv.at[zh], peer)
        cp.start()
        sent.append(cp)

    for i, j in enumerate(Z_FAR):
        w, peer = z_of(j)
        send(zb.at[w], zb.at[w], z_send.at[i], z_recv.at[w], peer).wait_recv()
    psum = zb[0]
    for w in range(1, 8):
        psum = psum + zb[w]
    cb[m] = psum
    for i, f in enumerate(OCT_FAR):
        q, peer = oct_of(f)
        cp = send(cb.at[m], cb.at[m], c8_send.at[i], c8_recv.at[m], peer)
        cp.start()
        sent.append(cp)

    for i, j in enumerate(Z_FAR):
        w, peer = z_of(j)
        send(gz.at[w], gz.at[w], gz_send.at[i], gz_recv.at[w], peer).wait_recv()
    gsum = gz[0]
    for w in range(1, 8):
        gsum = gsum + gz[w]
    row_id = lax.broadcasted_iota(jnp.int32, (K, 128), 0)
    lane_id = lax.broadcasted_iota(jnp.int32, (K, 128), 1)
    full = jnp.concatenate(
        [gsum] + [pltpu.roll(gsum, 128 - K * b, 1) for b in range(1, 4)], axis=0
    )
    eye = jnp.where(lane_id == row_id + K, 1.0, 0.0)
    mat = jnp.where(lane_id < K, full, eye)
    for k in range(K - 1):
        row = mat[k : k + 1, :]
        col = mat[:, k : k + 1] / mat[k : k + 1, k : k + 1]
        mat = mat - jnp.where(row_id > k, col * row, 0.0)
    diag = jnp.sum(jnp.where(lane_id == row_id, mat, 0.0), axis=1, keepdims=True)
    mat = mat * lax.rsqrt(diag)
    inverse = pltpu.roll(mat, 128 - K, 1)[:, :K]

    for i, f in enumerate(OCT_FAR):
        q, peer = oct_of(f)
        send(cb.at[q], cb.at[q], c8_send.at[i], c8_recv.at[q], peer).wait_recv()
    for q in range(8):
        coef_out[:, 128 * q : 128 * q + 128] = jnp.dot(
            inverse, cb[q], preferred_element_type=jnp.float32, precision=lax.Precision.HIGHEST
        )
    for cp in sent:
        cp.wait_send()
    for cp in outs:
        cp.wait()


def per_device(snapshots, omega):
    rows = snapshots.shape[0] // 8
    cols = snapshots.shape[1]
    f32, bf16 = jnp.float32, jnp.bfloat16
    dma = pltpu.SemaphoreType.DMA
    return pl.pallas_call(
        kernel,
        name="pod",
        out_shape=(
            jax.ShapeDtypeStruct((K, snapshots.shape[0]), bf16),
            jax.ShapeDtypeStruct((K, cols), f32),
        ),
        in_specs=[pl.BlockSpec(memory_space=pl.ANY)] * 2,
        out_specs=(
            pl.BlockSpec(memory_space=pl.ANY),
            pl.BlockSpec(memory_space=pltpu.VMEM),
        ),
        scratch_shapes=[
            pltpu.VMEM((8, rows, cols), bf16),
            pltpu.VMEM((K, cols), jnp.int32),
            pltpu.VMEM((8, K, rows), f32),
            pltpu.VMEM((7, K, rows), f32),
            pltpu.VMEM((8, K, rows), bf16),
            pltpu.VMEM((8, K, 128), f32),
            pltpu.VMEM((8, K, 128), f32),
            pltpu.VMEM((8, K, 128), f32),
            pltpu.VMEM((8, K, 128), f32),
            pltpu.VMEM((8, 8, 128), f32),
            pltpu.VMEM((8, 8, 128), f32),
            dma((8,)), dma, dma((8,)),
        ]
        + [dma((7,)), dma((7,))]
        + [dma((7,)), dma((8,))] * 6,
        compiler_params=pltpu.CompilerParams(collective_id=0, has_side_effects=True),
    )(snapshots, omega)


def solution(mesh):
    return jax.shard_map(
        per_device,
        mesh=mesh,
        in_specs=(P("space", "tm"), P(None, "tm")),
        out_specs=(P(None, "space"), P(None, "tm")),
        check_vma=False,
    )
```

```python
import jax
import jax.numpy as jnp
from jax import lax
from jax.experimental import pallas as pl
from jax.experimental.pallas import tpu as pltpu
from jax.sharding import PartitionSpec as P

MESH = pl.DeviceIdType.MESH
SNAP = 8192
K = 32
TM_FAR = ((1, 2), (1, 1), (1, 3), (1, 0), (0, 2), (0, 1), (0, 3))
OCT_FAR = ((1, 1, 0), (1, 1, 1), (1, 0, 0), (1, 0, 1), (0, 1, 0), (0, 1, 1), (0, 0, 1))
Z_FAR = (4, 3, 5, 2, 6, 1, 7)


def flip(bit, f):
    return (bit + f) % 2


def kernel(
    snap, omega, sk, coef,
    a, om, part, rs, pp, r8, zb, cb, g8, gz,
    in_sem, om_sem, near_sem, far_sem,
    rs_send, rs_recv, ag_send, ag_recv, p8_send, p8_recv, z_send, z_recv,
    c8_send, c8_recv, g8_send, g8_recv, gz_send, gz_recv,
):
    s, t = lax.axis_index("space"), lax.axis_index("tm")
    z, xl, c = s // 4, (s // 2) % 2, s % 2
    xh, y = t // 4, t % 4
    zh, zp = z // 2, z % 2
    m = zp * 4 + xl * 2 + c
    rows = a.shape[1]

    def tm_of(off):
        return flip(xh, off[0]) * 4 + (y + off[1]) % 4

    def oct_of(f):
        q = flip(zp, f[0]) * 4 + flip(xl, f[1]) * 2 + flip(c, f[2])
        return q, (zh * 8 + q, t)

    def z_of(j):
        w = (zh + j) % 8
        return w, (w * 8 + m, t)

    om_copy = pltpu.make_async_copy(omega, om, om_sem)
    om_copy.start()
    order = [tm_of(off) for off in TM_FAR] + [t]
    loads = []
    for i, d in enumerate(order):
        cp = pltpu.make_async_copy(
            snap.at[pl.ds(pl.multiple_of(d * rows, rows), rows), :], a.at[d], in_sem.at[i]
        )
        cp.start()
        loads.append(cp)

    barrier = pltpu.get_barrier_semaphore()
    peers = [(s, tm_of(off)) for off in TM_FAR]
    peers += [oct_of(f)[1] for f in OCT_FAR] + [z_of(j)[1] for j in (1, 7)]
    for peer in peers:
        pl.semaphore_signal(barrier, inc=1, device_id=peer, device_id_type=MESH)

    def tell(sem, steps):
        for j in steps:
            pl.semaphore_signal(sem, inc=1, device_id=z_of(j)[1], device_id_type=MESH)

    def rows_of(d):
        return sk.at[:, pl.ds(pl.multiple_of(d * rows, rows), rows)]

    def send(src, dst, send_sem, recv_sem, peer):
        return pltpu.make_async_remote_copy(
            src_ref=src, dst_ref=dst, send_sem=send_sem, recv_sem=recv_sem,
            device_id=peer, device_id_type=MESH,
        )

    om_copy.wait()
    signs = om[...].astype(jnp.float32).astype(jnp.bfloat16)
    sent = []
    rs_copies = []
    for i, d in enumerate(order):
        loads[i].wait()
        part[i] = lax.dot_general(
            signs, a[d], (((1,), (1,)), ((), ())), preferred_element_type=jnp.float32
        )
        if i == 0:
            pl.semaphore_wait(barrier, len(peers))
            tell(near_sem, (1, 7))
        if i < 7:
            cp = send(part.at[i], rs.at[i], rs_send.at[i], rs_recv.at[i], (s, d))
            cp.start()
            rs_copies.append(cp)
    sent += rs_copies
    pl.semaphore_wait(near_sem, 2)
    tell(far_sem, (2, 6))

    total = part[7]
    for i in (5, 6, 4, 3, 1, 2, 0):
        rs_copies[i].wait_recv()
        total = total + rs[i]
    factor = SNAP ** (-0.5)
    sk[:, pl.ds(pl.multiple_of(t * rows, rows), rows)] = (total * factor).astype(jnp.bfloat16)
    for i, off in enumerate(TM_FAR):
        cp = send(rows_of(t), rows_of(t), ag_send.at[i], ag_recv.at[t], (s, order[i]))
        cp.start()
        sent.append(cp)

    proj = None
    gram = None
    for i in (7, 5, 6, 4, 3, 1, 2, 0):
        d = order[i]
        if i < 7:
            send(rows_of(d), rows_of(d), ag_send.at[i], ag_recv.at[d], (s, d)).wait_recv()
        block = sk[:, pl.ds(pl.multiple_of(d * rows, rows), rows)]
        wide = jnp.concatenate([block] * 4, axis=0)
        g = lax.dot_general(
            block, wide, (((1,), (1,)), ((), ())), preferred_element_type=jnp.float32
        )
        p = jnp.dot(block, a[d], preferred_element_type=jnp.float32)
        gram = g if gram is None else gram + g
        proj = p if proj is None else proj + p

    lane8 = lax.broadcasted_iota(jnp.int32, (8, 128), 1) // K
    packed = jnp.zeros((8, 128), jnp.float32)
    for b in range(4):
        packed = jnp.where(lane8 == b, gram[8 * b : 8 * b + 8], packed)
    g8[m] = packed
    for i, f in enumerate(OCT_FAR):
        q, peer = oct_of(f)
        cp = send(g8.at[m], g8.at[m], g8_send.at[i], g8_recv.at[m], peer)
        cp.start()
        sent.append(cp)
    for q in range(8):
        pp[q] = proj[:, 128 * q : 128 * q + 128]
    r8[m] = pp[m]
    for i, f in enumerate(OCT_FAR):
        q, peer = oct_of(f)
        cp = send(pp.at[q], r8.at[m], p8_send.at[i], p8_recv.at[m], peer)
        cp.start()
        sent.append(cp)

    for i, f in enumerate(OCT_FAR):
        q, peer = oct_of(f)
        send(g8.at[q], g8.at[q], g8_send.at[i], g8_recv.at[q], peer).wait_recv()
    gsum = g8[0]
    for q in range(1, 8):
        gsum = gsum + g8[q]
    gz[zh] = gsum
    pl.semaphore_wait(far_sem, 2)
    for i, j in enumerate(Z_FAR):
        w, peer = z_of(j)
        cp = send(gz.at[zh], gz.at[zh], gz_send.at[i], gz_recv.at[zh], peer)
        cp.start()
        sent.append(cp)

    for i, f in enumerate(OCT_FAR):
        q, peer = oct_of(f)
        send(pp.at[q], r8.at[q], p8_send.at[i], p8_recv.at[q], peer).wait_recv()
    psum = r8[0]
    for q in range(1, 8):
        psum = psum + r8[q]
    zb[zh] = psum
    for i, j in enumerate(Z_FAR):
        w, peer = z_of(j)
        cp = send(zb.at[zh], zb.at[zh], z_send.at[i], z_recv.at[zh], peer)
        cp.start()
        sent.append(cp)

    for i, j in enumerate(Z_FAR):
        w, peer = z_of(j)
        send(gz.at[w], gz.at[w], gz_send.at[i], gz_recv.at[w], peer).wait_recv()
    gsum = gz[0]
    for w in range(1, 8):
        gsum = gsum + gz[w]
    row_id = lax.broadcasted_iota(jnp.int32, (K, 128), 0)
    lane_id = lax.broadcasted_iota(jnp.int32, (K, 128), 1)
    full = jnp.concatenate(
        [gsum] + [pltpu.roll(gsum, 128 - K * b, 1) for b in range(1, 4)], axis=0
    )
    eye = jnp.where(lane_id == row_id + K, 1.0, 0.0)
    mat = jnp.where(lane_id < K, full, eye)
    for k in range(K - 1):
        row = mat[k : k + 1, :]
        col = mat[:, k : k + 1] / mat[k : k + 1, k : k + 1]
        mat = mat - jnp.where(row_id > k, col * row, 0.0)
    diag = jnp.sum(jnp.where(lane_id == row_id, mat, 0.0), axis=1, keepdims=True)
    mat = mat * lax.rsqrt(diag)
    inverse = pltpu.roll(mat, 128 - K, 1)[:, :K]

    for i, j in enumerate(Z_FAR):
        w, peer = z_of(j)
        send(zb.at[w], zb.at[w], z_send.at[i], z_recv.at[w], peer).wait_recv()
    psum = zb[0]
    for w in range(1, 8):
        psum = psum + zb[w]
    cb[m] = jnp.dot(
        inverse, psum, preferred_element_type=jnp.float32, precision=lax.Precision.HIGHEST
    ).astype(jnp.bfloat16)
    for i, f in enumerate(OCT_FAR):
        q, peer = oct_of(f)
        cp = send(cb.at[m], cb.at[m], c8_send.at[i], c8_recv.at[m], peer)
        cp.start()
        sent.append(cp)

    for i, f in enumerate(OCT_FAR):
        q, peer = oct_of(f)
        send(cb.at[q], cb.at[q], c8_send.at[i], c8_recv.at[q], peer).wait_recv()
    for q in range(8):
        coef[:, 128 * q : 128 * q + 128] = cb[q].astype(jnp.float32)
    for cp in sent:
        cp.wait_send()


def per_device(snapshots, omega):
    rows = snapshots.shape[0] // 8
    cols = snapshots.shape[1]
    f32, bf16 = jnp.float32, jnp.bfloat16
    dma, regular = pltpu.SemaphoreType.DMA, pltpu.SemaphoreType.REGULAR
    whole = pl.BlockSpec(memory_space=pltpu.VMEM)
    return pl.pallas_call(
        kernel,
        name="pod",
        out_shape=(
            pltpu.VMEM((K, snapshots.shape[0]), bf16),
            pltpu.VMEM((K, cols), f32),
        ),
        in_specs=[pl.BlockSpec(memory_space=pltpu.HBM)] * 2,
        out_specs=(whole, whole),
        scratch_shapes=[
            pltpu.VMEM((8, rows, cols), bf16),
            pltpu.VMEM((K, cols), jnp.int32),
            pltpu.VMEM((8, K, rows), f32),
            pltpu.VMEM((7, K, rows), f32),
            pltpu.VMEM((8, K, 128), f32),
            pltpu.VMEM((8, K, 128), f32),
            pltpu.VMEM((8, K, 128), f32),
            pltpu.VMEM((8, K, 128), bf16),
            pltpu.VMEM((8, 8, 128), f32),
            pltpu.VMEM((8, 8, 128), f32),
            dma((8,)), dma, regular, regular,
        ]
        + [dma((7,)), dma((7,))]
        + [dma((7,)), dma((8,))] * 6,
        compiler_params=pltpu.CompilerParams(
            collective_id=0, has_side_effects=True, vmem_limit_bytes=48 * 2**20
        ),
    )(
        pltpu.with_memory_space_constraint(snapshots, pltpu.HBM),
        pltpu.with_memory_space_constraint(omega, pltpu.HBM),
    )

def solution(mesh):
    return jax.shard_map(
        per_device,
        mesh=mesh,
        in_specs=(P("space", "tm"), P(None, "tm")),
        out_specs=(P(None, "space"), P(None, "tm")),
        check_vma=False,
    )
```

```python
import jax
import jax.numpy as jnp
from jax import lax
from jax.experimental import pallas as pl
from jax.experimental.pallas import tpu as pltpu
from jax.sharding import PartitionSpec as P

MESH = pl.DeviceIdType.MESH
SNAP = 8192
K = 32
TM_FAR = ((1, 2), (1, 1), (1, 3), (1, 0), (0, 2), (0, 1), (0, 3))
OCT_FAR = ((1, 1, 0), (1, 1, 1), (1, 0, 0), (1, 0, 1), (0, 1, 0), (0, 1, 1), (0, 0, 1))
Z_FAR = (4, 3, 5, 2, 6, 1, 7)


def flip(bit, f):
    return (bit + f) % 2


def to_int16(x):
    top = jnp.max(jnp.max(jnp.abs(x), axis=0, keepdims=True), axis=1, keepdims=True)
    top = jnp.where(top > 0.0, top, 1.0)
    units = jnp.round(x * (32766.0 / top)).astype(jnp.int32).astype(jnp.int16)
    return units, jnp.broadcast_to(top * (1.0 / 32766.0), (1, 128))


def from_int16(units, step):
    return units.astype(jnp.int32).astype(jnp.float32) * step


def kernel(
    snap, omega, sk, coef,
    a, om, part, rs, pp, r8, rst, zb, zs, cb, g8, gz,
    in_sem, om_sem, near_sem, far_sem,
    rs_send, rs_recv, ag_send, ag_recv, p8_send, p8_recv, z_send, z_recv,
    c8_send, c8_recv, g8_send, g8_recv, gz_send, gz_recv, zs_send, zs_recv, rst_send, rst_recv,
):
    s, t = lax.axis_index("space"), lax.axis_index("tm")
    z, xl, c = s // 4, (s // 2) % 2, s % 2
    xh, y = t // 4, t % 4
    zh, zp = z // 2, z % 2
    m = zp * 4 + xl * 2 + c
    rows = a.shape[1]

    def tm_of(off):
        return flip(xh, off[0]) * 4 + (y + off[1]) % 4

    def oct_of(f):
        q = flip(zp, f[0]) * 4 + flip(xl, f[1]) * 2 + flip(c, f[2])
        return q, (zh * 8 + q, t)

    def z_of(j):
        w = (zh + j) % 8
        return w, (w * 8 + m, t)

    om_copy = pltpu.make_async_copy(omega, om, om_sem)
    om_copy.start()
    barrier = pltpu.get_barrier_semaphore()
    peers = [(s, tm_of(off)) for off in TM_FAR]
    peers += [oct_of(f)[1] for f in OCT_FAR] + [z_of(j)[1] for j in (1, 7)]
    for peer in peers:
        pl.semaphore_signal(barrier, inc=1, device_id=peer, device_id_type=MESH)

    order = [tm_of(off) for off in TM_FAR] + [t]
    loads = [
        pltpu.make_async_copy(
            snap.at[pl.ds(pl.multiple_of(d * rows, rows), rows), :], a.at[d], in_sem.at[i]
        )
        for i, d in enumerate(order)
    ]
    for cp in loads[:4]:
        cp.start()

    def tell(sem, steps):
        for j in steps:
            pl.semaphore_signal(sem, inc=1, device_id=z_of(j)[1], device_id_type=MESH)

    def rows_of(d):
        return sk.at[:, pl.ds(pl.multiple_of(d * rows, rows), rows)]

    def send(src, dst, send_sem, recv_sem, peer):
        return pltpu.make_async_remote_copy(
            src_ref=src, dst_ref=dst, send_sem=send_sem, recv_sem=recv_sem,
            device_id=peer, device_id_type=MESH,
        )

    om_copy.wait()
    for cp in loads[4:]:
        cp.start()
    signs = om[...].astype(jnp.float32).astype(jnp.bfloat16)
    sent = []
    rs_copies = []
    for first in (0, 4):
        for i in range(first, first + 4):
            loads[i].wait()
        for i in range(first, first + 4):
            part[i] = lax.dot_general(
                signs, a[order[i]], (((1,), (1,)), ((), ())), preferred_element_type=jnp.float32
            )
        if first == 0:
            pl.semaphore_wait(barrier, len(peers))
            tell(near_sem, (1, 7))
        for i in range(first, min(first + 4, 7)):
            cp = send(part.at[i], rs.at[i], rs_send.at[i], rs_recv.at[i], (s, order[i]))
            cp.start()
            rs_copies.append(cp)
    sent += rs_copies
    pl.semaphore_wait(near_sem, 2)
    tell(far_sem, (2, 6))

    total = part[7]
    for i in (5, 6, 4, 3, 1, 2, 0):
        rs_copies[i].wait_recv()
        total = total + rs[i]
    factor = SNAP ** (-0.5)
    sk[:, pl.ds(pl.multiple_of(t * rows, rows), rows)] = (total * factor).astype(jnp.bfloat16)
    for i, off in enumerate(TM_FAR):
        cp = send(rows_of(t), rows_of(t), ag_send.at[i], ag_recv.at[t], (s, order[i]))
        cp.start()
        sent.append(cp)

    proj = None
    gram = None
    for i in (7, 5, 6, 4, 3, 1, 2, 0):
        d = order[i]
        if i < 7:
            send(rows_of(d), rows_of(d), ag_send.at[i], ag_recv.at[d], (s, d)).wait_recv()
        block = sk[:, pl.ds(pl.multiple_of(d * rows, rows), rows)]
        wide = jnp.concatenate([block] * 4, axis=0)
        g = lax.dot_general(
            block, wide, (((1,), (1,)), ((), ())), preferred_element_type=jnp.float32
        )
        p = jnp.dot(block, a[d], preferred_element_type=jnp.float32)
        gram = g if gram is None else gram + g
        proj = p if proj is None else proj + p

    lane8 = lax.broadcasted_iota(jnp.int32, (8, 128), 1) // K
    packed = jnp.zeros((8, 128), jnp.float32)
    for b in range(4):
        packed = jnp.where(lane8 == b, gram[8 * b : 8 * b + 8], packed)
    g8[m] = packed
    for i, f in enumerate(OCT_FAR):
        q, peer = oct_of(f)
        cp = send(g8.at[m], g8.at[m], g8_send.at[i], g8_recv.at[m], peer)
        cp.start()
        sent.append(cp)
    units, rst[m] = to_int16(proj)
    for q in range(8):
        pp[q] = units[:, 128 * q : 128 * q + 128]
    r8[m] = pp[m]
    for i, f in enumerate(OCT_FAR):
        q, peer = oct_of(f)
        cp = send(pp.at[q], r8.at[m], p8_send.at[i], p8_recv.at[m], peer)
        cp.start()
        sent.append(cp)
        cp = send(rst.at[m], rst.at[m], rst_send.at[i], rst_recv.at[m], peer)
        cp.start()
        sent.append(cp)

    for i, f in enumerate(OCT_FAR):
        q, peer = oct_of(f)
        send(g8.at[q], g8.at[q], g8_send.at[i], g8_recv.at[q], peer).wait_recv()
    gsum = g8[0]
    for q in range(1, 8):
        gsum = gsum + g8[q]
    gz[zh] = gsum
    pl.semaphore_wait(far_sem, 2)
    for i, j in enumerate(Z_FAR):
        w, peer = z_of(j)
        cp = send(gz.at[zh], gz.at[zh], gz_send.at[i], gz_recv.at[zh], peer)
        cp.start()
        sent.append(cp)

    for i, f in enumerate(OCT_FAR):
        q, peer = oct_of(f)
        send(pp.at[q], r8.at[q], p8_send.at[i], p8_recv.at[q], peer).wait_recv()
        send(rst.at[q], rst.at[q], rst_send.at[i], rst_recv.at[q], peer).wait_recv()
    psum = from_int16(r8[0], rst[0])
    for q in range(1, 8):
        psum = psum + from_int16(r8[q], rst[q])
    zb[zh], zs[zh] = to_int16(psum)
    for i, j in enumerate(Z_FAR):
        w, peer = z_of(j)
        cp = send(zb.at[zh], zb.at[zh], z_send.at[i], z_recv.at[zh], peer)
        cp.start()
        sent.append(cp)
        cp = send(zs.at[zh], zs.at[zh], zs_send.at[i], zs_recv.at[zh], peer)
        cp.start()
        sent.append(cp)

    for i, j in enumerate(Z_FAR):
        w, peer = z_of(j)
        send(gz.at[w], gz.at[w], gz_send.at[i], gz_recv.at[w], peer).wait_recv()
    gsum = gz[0]
    for w in range(1, 8):
        gsum = gsum + gz[w]
    row_id = lax.broadcasted_iota(jnp.int32, (K, 128), 0)
    lane_id = lax.broadcasted_iota(jnp.int32, (K, 128), 1)
    full = jnp.concatenate(
        [gsum] + [pltpu.roll(gsum, 128 - K * b, 1) for b in range(1, 4)], axis=0
    )
    eye = jnp.where(lane_id == row_id + K, 1.0, 0.0)
    mat = jnp.where(lane_id < K, full, eye)
    for panel in range(0, K, 8):
        cols = [
            jnp.broadcast_to(mat[:, k : k + 1], (K, 128)) for k in range(panel, panel + 8)
        ]
        for j in range(8):
            k = panel + j
            ratio = jnp.where(row_id > k, cols[j] * (1.0 / cols[j][k : k + 1, :]), 0.0)
            for l in range(j + 1, 8):
                cols[l] = cols[l] - ratio * cols[l][k : k + 1, :]
            mat = mat - ratio * mat[k : k + 1, :]
    diag = jnp.sum(jnp.where(lane_id == row_id, mat, 0.0), axis=1, keepdims=True)
    mat = mat * lax.rsqrt(diag)
    inverse = pltpu.roll(mat, 128 - K, 1)[:, :K]

    for i, j in enumerate(Z_FAR):
        w, peer = z_of(j)
        send(zb.at[w], zb.at[w], z_send.at[i], z_recv.at[w], peer).wait_recv()
        send(zs.at[w], zs.at[w], zs_send.at[i], zs_recv.at[w], peer).wait_recv()
    psum = from_int16(zb[0], zs[0])
    for w in range(1, 8):
        psum = psum + from_int16(zb[w], zs[w])
    cb[m] = jnp.dot(
        inverse, psum, preferred_element_type=jnp.float32, precision=lax.Precision.HIGHEST
    ).astype(jnp.bfloat16)
    for i, f in enumerate(OCT_FAR):
        q, peer = oct_of(f)
        cp = send(cb.at[m], cb.at[m], c8_send.at[i], c8_recv.at[m], peer)
        cp.start()
        sent.append(cp)

    for i, f in enumerate(OCT_FAR):
        q, peer = oct_of(f)
        send(cb.at[q], cb.at[q], c8_send.at[i], c8_recv.at[q], peer).wait_recv()
    for q in range(8):
        coef[:, 128 * q : 128 * q + 128] = cb[q].astype(jnp.float32)
    for cp in sent:
        cp.wait_send()


def store(sk, coef, sketch_out, coef_out, sem):
    copies = [
        pltpu.make_async_copy(sk, sketch_out, sem.at[0]),
        pltpu.make_async_copy(coef, coef_out, sem.at[1]),
    ]
    for cp in copies:
        cp.start()
    for cp in copies:
        cp.wait()


def per_device(snapshots, omega):
    rows = snapshots.shape[0] // 8
    cols = snapshots.shape[1]
    f32, bf16 = jnp.float32, jnp.bfloat16
    dma, regular = pltpu.SemaphoreType.DMA, pltpu.SemaphoreType.REGULAR
    whole = pl.BlockSpec(memory_space=pltpu.VMEM)
    sk, coef = pl.pallas_call(
        kernel,
        name="pod",
        out_shape=(
            pltpu.VMEM((K, snapshots.shape[0]), bf16),
            pltpu.VMEM((K, cols), f32),
        ),
        in_specs=[pl.BlockSpec(memory_space=pltpu.HBM)] * 2,
        out_specs=(whole, whole),
        scratch_shapes=[
            pltpu.VMEM((8, rows, cols), bf16),
            pltpu.VMEM((K, cols), jnp.int32),
            pltpu.VMEM((8, K, rows), f32),
            pltpu.VMEM((7, K, rows), f32),
            pltpu.VMEM((8, K, 128), jnp.int16),
            pltpu.VMEM((8, K, 128), jnp.int16),
            pltpu.VMEM((8, 1, 128), f32),
            pltpu.VMEM((8, K, 128), jnp.int16),
            pltpu.VMEM((8, 1, 128), f32),
            pltpu.VMEM((8, K, 128), bf16),
            pltpu.VMEM((8, 8, 128), f32),
            pltpu.VMEM((8, 8, 128), f32),
            dma((8,)), dma, regular, regular,
        ]
        + [dma((7,)), dma((7,))]
        + [dma((7,)), dma((8,))] * 8,
        compiler_params=pltpu.CompilerParams(
            collective_id=0, has_side_effects=True, vmem_limit_bytes=48 * 2**20
        ),
    )(
        pltpu.with_memory_space_constraint(snapshots, pltpu.HBM),
        pltpu.with_memory_space_constraint(omega, pltpu.HBM),
    )
    return pl.pallas_call(
        store,
        name="store",
        out_shape=(
            jax.ShapeDtypeStruct(sk.shape, sk.dtype),
            jax.ShapeDtypeStruct(coef.shape, coef.dtype),
        ),
        in_specs=[whole] * 2,
        out_specs=(pl.BlockSpec(memory_space=pl.ANY),) * 2,
        scratch_shapes=[dma((2,))],
        compiler_params=pltpu.CompilerParams(vmem_limit_bytes=4 * 2**20),
    )(sk, coef)

def solution(mesh):
    return jax.shard_map(
        per_device,
        mesh=mesh,
        in_specs=(P("space", "tm"), P(None, "tm")),
        out_specs=(P(None, "space"), P(None, "tm")),
        check_vma=False,
    )
```

```python
import jax
import jax.numpy as jnp
from jax import lax
from jax.experimental import pallas as pl
from jax.experimental.pallas import tpu as pltpu
from jax.sharding import PartitionSpec as P

MESH = pl.DeviceIdType.MESH
SNAP = 8192
K = 32
TM_FAR = ((1, 2), (1, 1), (1, 3), (1, 0), (0, 2), (0, 1), (0, 3))
OCT_FAR = ((1, 1, 0), (1, 1, 1), (1, 0, 0), (1, 0, 1), (0, 1, 0), (0, 1, 1), (0, 0, 1))
Z_FAR = (4, 3, 5, 2, 6, 1, 7)


def flip(bit, f):
    return (bit + f) % 2


def to_int16(x):
    top = jnp.max(jnp.max(jnp.abs(x), axis=0, keepdims=True), axis=1, keepdims=True)
    top = jnp.where(top > 0.0, top, 1.0)
    units = jnp.round(x * (32766.0 / top)).astype(jnp.int32).astype(jnp.int16)
    return units, jnp.broadcast_to(top * (1.0 / 32766.0), (1, 128))


def from_int16(units, step):
    return units.astype(jnp.int32).astype(jnp.float32) * step


def kernel(
    snap, omega, sk, coef,
    a, om, part, rs, pp, r8, rst, zb, zs, cb, g8, gz,
    in_sem, om_sem, near_sem, far_sem,
    rs_send, rs_recv, ag_send, ag_recv, p8_send, p8_recv, z_send, z_recv,
    c8_send, c8_recv, g8_send, g8_recv, gz_send, gz_recv, zs_send, zs_recv, rst_send, rst_recv,
):
    s, t = lax.axis_index("space"), lax.axis_index("tm")
    z, xl, c = s // 4, (s // 2) % 2, s % 2
    xh, y = t // 4, t % 4
    zh, zp = z // 2, z % 2
    m = zp * 4 + xl * 2 + c
    rows = a.shape[1]

    def tm_of(off):
        return flip(xh, off[0]) * 4 + (y + off[1]) % 4

    def oct_of(f):
        q = flip(zp, f[0]) * 4 + flip(xl, f[1]) * 2 + flip(c, f[2])
        return q, (zh * 8 + q, t)

    def z_of(j):
        w = (zh + j) % 8
        return w, (w * 8 + m, t)

    om_copy = pltpu.make_async_copy(omega, om, om_sem)
    om_copy.start()
    barrier = pltpu.get_barrier_semaphore()
    peers = [(s, tm_of(off)) for off in TM_FAR]
    peers += [oct_of(f)[1] for f in OCT_FAR] + [z_of(j)[1] for j in (1, 7)]
    for peer in peers:
        pl.semaphore_signal(barrier, inc=1, device_id=peer, device_id_type=MESH)

    order = [tm_of(off) for off in TM_FAR] + [t]
    loads = [
        pltpu.make_async_copy(
            snap.at[pl.ds(pl.multiple_of(d * rows, rows), rows), :], a.at[d], in_sem.at[i // 4]
        )
        for i, d in enumerate(order)
    ]
    for cp in loads[:4]:
        cp.start()

    def tell(sem, steps):
        for j in steps:
            pl.semaphore_signal(sem, inc=1, device_id=z_of(j)[1], device_id_type=MESH)

    def rows_of(d):
        return sk.at[:, pl.ds(pl.multiple_of(d * rows, rows), rows)]

    def send(src, dst, send_sem, recv_sem, peer):
        return pltpu.make_async_remote_copy(
            src_ref=src, dst_ref=dst, send_sem=send_sem, recv_sem=recv_sem,
            device_id=peer, device_id_type=MESH,
        )

    def arrived(blocks, send_sem, recv_sem):
        send(blocks, blocks, send_sem, recv_sem, peers[0]).wait_recv()

    def left(blocks, send_sem, recv_sem):
        send(blocks, blocks, send_sem, recv_sem, peers[0]).wait_send()

    om_copy.wait()
    for cp in loads[4:]:
        cp.start()
    signs = om[...].astype(jnp.float32).astype(jnp.bfloat16)
    for first in (0, 4):
        four = a.at[pl.ds(0, 4)]
        pltpu.make_async_copy(four, four, in_sem.at[first // 4]).wait()
        for i in range(first, first + 4):
            part[i] = lax.dot_general(
                signs, a[order[i]], (((1,), (1,)), ((), ())), preferred_element_type=jnp.float32
            )
        if first == 0:
            pl.semaphore_wait(barrier, len(peers))
            tell(near_sem, (1, 7))
        for i in range(first, min(first + 4, 7)):
            cp = send(part.at[i], rs.at[i], rs_send, rs_recv, (s, order[i]))
            cp.start()
    pl.semaphore_wait(near_sem, 2)
    tell(far_sem, (2, 6))

    total = part[7]
    arrived(rs, rs_send, rs_recv)
    for i in range(7):
        total = total + rs[i]
    factor = SNAP ** (-0.5)
    sk[:, pl.ds(pl.multiple_of(t * rows, rows), rows)] = (total * factor).astype(jnp.bfloat16)
    for i, off in enumerate(TM_FAR):
        cp = send(rows_of(t), rows_of(t), ag_send, ag_recv.at[t], (s, order[i]))
        cp.start()

    proj = None
    gram = None
    for i in (7, 5, 6, 4, 3, 1, 2, 0):
        d = order[i]
        if i < 7:
            send(rows_of(d), rows_of(d), ag_send, ag_recv.at[d], (s, d)).wait_recv()
        block = sk[:, pl.ds(pl.multiple_of(d * rows, rows), rows)]
        wide = jnp.concatenate([block] * 4, axis=0)
        g = lax.dot_general(
            block, wide, (((1,), (1,)), ((), ())), preferred_element_type=jnp.float32
        )
        p = jnp.dot(block, a[d], preferred_element_type=jnp.float32)
        gram = g if gram is None else gram + g
        proj = p if proj is None else proj + p

    lane8 = lax.broadcasted_iota(jnp.int32, (8, 128), 1) // K
    packed = jnp.zeros((8, 128), jnp.float32)
    for b in range(4):
        packed = jnp.where(lane8 == b, gram[8 * b : 8 * b + 8], packed)
    g8[m] = packed
    for i, f in enumerate(OCT_FAR):
        q, peer = oct_of(f)
        cp = send(g8.at[m], g8.at[m], g8_send, g8_recv, peer)
        cp.start()
    units, rst[m] = to_int16(proj)
    for q in range(8):
        pp[q] = units[:, 128 * q : 128 * q + 128]
    r8[m] = pp[m]
    for i, f in enumerate(OCT_FAR):
        q, peer = oct_of(f)
        cp = send(pp.at[q], r8.at[m], p8_send, p8_recv, peer)
        cp.start()
        cp = send(rst.at[m], rst.at[m], rst_send, rst_recv, peer)
        cp.start()

    arrived(g8.at[pl.ds(0, 7)], g8_send, g8_recv)
    gsum = g8[0]
    for q in range(1, 8):
        gsum = gsum + g8[q]
    gz[zh] = gsum
    pl.semaphore_wait(far_sem, 2)
    for i, j in enumerate(Z_FAR):
        w, peer = z_of(j)
        cp = send(gz.at[zh], gz.at[zh], gz_send, gz_recv, peer)
        cp.start()

    arrived(r8.at[pl.ds(0, 7)], p8_send, p8_recv)
    arrived(rst.at[pl.ds(0, 7)], rst_send, rst_recv)
    psum = from_int16(r8[0], rst[0])
    for q in range(1, 8):
        psum = psum + from_int16(r8[q], rst[q])
    zb[zh], zs[zh] = to_int16(psum)
    for i, j in enumerate(Z_FAR):
        w, peer = z_of(j)
        cp = send(zb.at[zh], zb.at[zh], z_send, z_recv, peer)
        cp.start()
        cp = send(zs.at[zh], zs.at[zh], zs_send, zs_recv, peer)
        cp.start()

    arrived(gz.at[pl.ds(0, 7)], gz_send, gz_recv)
    gsum = gz[0]
    for w in range(1, 8):
        gsum = gsum + gz[w]
    row_id = lax.broadcasted_iota(jnp.int32, (K, 128), 0)
    lane_id = lax.broadcasted_iota(jnp.int32, (K, 128), 1)
    full = jnp.concatenate(
        [gsum] + [pltpu.roll(gsum, 128 - K * b, 1) for b in range(1, 4)], axis=0
    )
    eye = jnp.where(lane_id == row_id + K, 1.0, 0.0)
    mat = jnp.where(lane_id < K, full, eye)
    for panel in range(0, K, 8):
        cols = [
            jnp.broadcast_to(mat[:, k : k + 1], (K, 128)) for k in range(panel, panel + 8)
        ]
        for j in range(8):
            k = panel + j
            ratio = jnp.where(row_id > k, cols[j] * (1.0 / cols[j][k : k + 1, :]), 0.0)
            for l in range(j + 1, 8):
                cols[l] = cols[l] - ratio * cols[l][k : k + 1, :]
            mat = mat - ratio * mat[k : k + 1, :]
    diag = jnp.sum(jnp.where(lane_id == row_id, mat, 0.0), axis=1, keepdims=True)
    mat = mat * lax.rsqrt(diag)
    inverse = pltpu.roll(mat, 128 - K, 1)[:, :K]

    arrived(zb.at[pl.ds(0, 7)], z_send, z_recv)
    arrived(zs.at[pl.ds(0, 7)], zs_send, zs_recv)
    psum = from_int16(zb[0], zs[0])
    for w in range(1, 8):
        psum = psum + from_int16(zb[w], zs[w])
    cb[m] = jnp.dot(
        inverse, psum, preferred_element_type=jnp.float32, precision=lax.Precision.HIGHEST
    ).astype(jnp.bfloat16)
    for i, f in enumerate(OCT_FAR):
        q, peer = oct_of(f)
        cp = send(cb.at[m], cb.at[m], c8_send, c8_recv, peer)
        cp.start()

    arrived(cb.at[pl.ds(0, 7)], c8_send, c8_recv)
    for q in range(8):
        coef[:, 128 * q : 128 * q + 128] = cb[q].astype(jnp.float32)
    left(rs, rs_send, rs_recv)
    left(sk.at[:, pl.ds(0, 7 * rows)], ag_send, ag_recv.at[0])
    for blocks, send_sem, recv_sem in (
        (g8, g8_send, g8_recv), (pp, p8_send, p8_recv), (rst, rst_send, rst_recv),
        (gz, gz_send, gz_recv), (zb, z_send, z_recv), (zs, zs_send, zs_recv), (cb, c8_send, c8_recv),
    ):
        left(blocks.at[pl.ds(0, 7)], send_sem, recv_sem)


def store(sk, coef, sketch_out, coef_out, sem):
    copies = [
        pltpu.make_async_copy(sk, sketch_out, sem.at[0]),
        pltpu.make_async_copy(coef, coef_out, sem.at[1]),
    ]
    for cp in copies:
        cp.start()
    for cp in copies:
        cp.wait()


def per_device(snapshots, omega):
    rows = snapshots.shape[0] // 8
    cols = snapshots.shape[1]
    f32, bf16 = jnp.float32, jnp.bfloat16
    dma, regular = pltpu.SemaphoreType.DMA, pltpu.SemaphoreType.REGULAR
    whole = pl.BlockSpec(memory_space=pltpu.VMEM)
    sk, coef = pl.pallas_call(
        kernel,
        name="pod",
        out_shape=(
            pltpu.VMEM((K, snapshots.shape[0]), bf16),
            pltpu.VMEM((K, cols), f32),
        ),
        in_specs=[pl.BlockSpec(memory_space=pltpu.HBM)] * 2,
        out_specs=(whole, whole),
        scratch_shapes=[
            pltpu.VMEM((8, rows, cols), bf16),
            pltpu.VMEM((K, cols), jnp.int32),
            pltpu.VMEM((8, K, rows), f32),
            pltpu.VMEM((7, K, rows), f32),
            pltpu.VMEM((8, K, 128), jnp.int16),
            pltpu.VMEM((8, K, 128), jnp.int16),
            pltpu.VMEM((8, 1, 128), f32),
            pltpu.VMEM((8, K, 128), jnp.int16),
            pltpu.VMEM((8, 1, 128), f32),
            pltpu.VMEM((8, K, 128), bf16),
            pltpu.VMEM((8, 8, 128), f32),
            pltpu.VMEM((8, 8, 128), f32),
            dma((2,)), dma, regular, regular,
        ]
        + [dma, dma, dma, dma((8,))]
        + [dma] * 14,
        compiler_params=pltpu.CompilerParams(
            collective_id=0, has_side_effects=True, vmem_limit_bytes=48 * 2**20
        ),
    )(
        pltpu.with_memory_space_constraint(snapshots, pltpu.HBM),
        pltpu.with_memory_space_constraint(omega, pltpu.HBM),
    )
    return pl.pallas_call(
        store,
        name="store",
        out_shape=(
            jax.ShapeDtypeStruct(sk.shape, sk.dtype),
            jax.ShapeDtypeStruct(coef.shape, coef.dtype),
        ),
        in_specs=[whole] * 2,
        out_specs=(pl.BlockSpec(memory_space=pl.ANY),) * 2,
        scratch_shapes=[dma((2,))],
        compiler_params=pltpu.CompilerParams(vmem_limit_bytes=4 * 2**20),
    )(sk, coef)

def solution(mesh):
    return jax.shard_map(
        per_device,
        mesh=mesh,
        in_specs=(P("space", "tm"), P(None, "tm")),
        out_specs=(P(None, "space"), P(None, "tm")),
        check_vma=False,
    )
```

```python
import jax
import jax.numpy as jnp
from jax import lax
from jax.experimental import pallas as pl
from jax.experimental.pallas import tpu as pltpu
from jax.sharding import PartitionSpec as P

MESH = pl.DeviceIdType.MESH
SNAP = 8192
K = 32
TM_FAR = ((1, 2), (1, 1), (1, 3), (1, 0), (0, 2), (0, 1), (0, 3))
OCT_FAR = ((1, 1, 0), (1, 1, 1), (1, 0, 0), (1, 0, 1), (0, 1, 0), (0, 1, 1), (0, 0, 1))
Z_FAR = (4, 3, 5, 2, 6, 1, 7)


def flip(bit, f):
    return (bit + f) % 2


def to_int16(x):
    top = jnp.max(jnp.max(jnp.abs(x), axis=0, keepdims=True), axis=1, keepdims=True)
    top = jnp.where(top > 0.0, top, 1.0)
    units = jnp.round(x * (32766.0 / top)).astype(jnp.int32).astype(jnp.int16)
    return units, jnp.broadcast_to(top * (1.0 / 32766.0), (1, 128))


def from_int16(units, step):
    return units.astype(jnp.int32).astype(jnp.float32) * step


def kernel(
    snap, omega, sk, coef,
    a, om, part, rs, pp, r8, rst, zb, zs, cb, g8, gz, gt,
    in_sem, om_sem, near_sem, far_sem,
    rs_send, rs_recv, ag_send, ag_recv, p8_send, p8_recv, z_send, z_recv,
    c8_send, c8_recv, g8_send, g8_recv, gz_send, gz_recv, zs_send, zs_recv, rst_send, rst_recv, gt_send, gt_recv,
):
    s, t = lax.axis_index("space"), lax.axis_index("tm")
    z, xl, c = s // 4, (s // 2) % 2, s % 2
    xh, y = t // 4, t % 4
    zh, zp = z // 2, z % 2
    m = zp * 4 + xl * 2 + c
    rows = a.shape[1]

    def tm_of(off):
        return flip(xh, off[0]) * 4 + (y + off[1]) % 4

    def oct_of(f):
        q = flip(zp, f[0]) * 4 + flip(xl, f[1]) * 2 + flip(c, f[2])
        return q, (zh * 8 + q, t)

    def z_of(j):
        w = (zh + j) % 8
        return w, (w * 8 + m, t)

    om_copy = pltpu.make_async_copy(omega, om, om_sem)
    om_copy.start()
    barrier = pltpu.get_barrier_semaphore()
    peers = [(s, tm_of(off)) for off in TM_FAR]
    peers += [oct_of(f)[1] for f in OCT_FAR] + [z_of(j)[1] for j in (1, 7)]
    for peer in peers:
        pl.semaphore_signal(barrier, inc=1, device_id=peer, device_id_type=MESH)

    order = [tm_of(off) for off in TM_FAR] + [t]
    loads = [
        pltpu.make_async_copy(
            snap.at[pl.ds(pl.multiple_of(d * rows, rows), rows), :], a.at[d], in_sem.at[i // 4]
        )
        for i, d in enumerate(order)
    ]
    for cp in loads[:4]:
        cp.start()

    def tell(sem, steps):
        for j in steps:
            pl.semaphore_signal(sem, inc=1, device_id=z_of(j)[1], device_id_type=MESH)

    def rows_of(d):
        return sk.at[:, pl.ds(pl.multiple_of(d * rows, rows), rows)]

    def send(src, dst, send_sem, recv_sem, peer):
        return pltpu.make_async_remote_copy(
            src_ref=src, dst_ref=dst, send_sem=send_sem, recv_sem=recv_sem,
            device_id=peer, device_id_type=MESH,
        )

    def arrived(blocks, send_sem, recv_sem):
        send(blocks, blocks, send_sem, recv_sem, peers[0]).wait_recv()

    def left(blocks, send_sem, recv_sem):
        send(blocks, blocks, send_sem, recv_sem, peers[0]).wait_send()

    om_copy.wait()
    for cp in loads[4:]:
        cp.start()
    signs = om[...].astype(jnp.float32).astype(jnp.bfloat16)
    for first in (0, 4):
        four = a.at[pl.ds(0, 4)]
        pltpu.make_async_copy(four, four, in_sem.at[first // 4]).wait()
        for i in range(first, first + 4):
            part[i] = lax.dot_general(
                signs, a[order[i]], (((1,), (1,)), ((), ())), preferred_element_type=jnp.float32
            )
        if first == 0:
            pl.semaphore_wait(barrier, len(peers))
            tell(near_sem, (1, 7))
        for i in range(first, min(first + 4, 7)):
            cp = send(part.at[i], rs.at[i], rs_send, rs_recv, (s, order[i]))
            cp.start()
    pl.semaphore_wait(near_sem, 2)
    tell(far_sem, (2, 6))

    total = part[7]
    arrived(rs, rs_send, rs_recv)
    for i in range(7):
        total = total + rs[i]
    factor = SNAP ** (-0.5)
    sk[:, pl.ds(pl.multiple_of(t * rows, rows), rows)] = (total * factor).astype(jnp.bfloat16)
    for i in range(7):
        peer = order[i] + c * (order[(i + 4) % 7] - order[i])
        cp = send(rows_of(t), rows_of(t), ag_send, ag_recv.at[t], (s, peer))
        cp.start()

    proj = None
    gram = None
    for i in (7, 5, 6, 4, 3, 1, 2, 0):
        d = order[i]
        if i < 7:
            send(rows_of(d), rows_of(d), ag_send, ag_recv.at[d], (s, d)).wait_recv()
        block = sk[:, pl.ds(pl.multiple_of(d * rows, rows), rows)]
        wide = jnp.concatenate([block] * 4, axis=0)
        g = lax.dot_general(
            block, wide, (((1,), (1,)), ((), ())), preferred_element_type=jnp.float32
        )
        p = jnp.dot(block, a[d], preferred_element_type=jnp.float32)
        gram = g if gram is None else gram + g
        proj = p if proj is None else proj + p

    lane8 = lax.broadcasted_iota(jnp.int32, (8, 128), 1) // K
    packed = jnp.zeros((8, 128), jnp.float32)
    for b in range(4):
        packed = jnp.where(lane8 == b, gram[8 * b : 8 * b + 8], packed)
    g8[m] = packed
    for i, f in enumerate(OCT_FAR):
        q, peer = oct_of(f)
        cp = send(g8.at[m], g8.at[m], g8_send, g8_recv, peer)
        cp.start()
    units, rst[m] = to_int16(proj)
    for q in range(8):
        pp[q] = units[:, 128 * q : 128 * q + 128]
    r8[m] = pp[m]
    for i, f in enumerate(OCT_FAR):
        q, peer = oct_of(f)
        cp = send(pp.at[q], r8.at[m], p8_send, p8_recv, peer)
        cp.start()
        cp = send(rst.at[m], rst.at[m], rst_send, rst_recv, peer)
        cp.start()

    arrived(g8.at[pl.ds(0, 7)], g8_send, g8_recv)
    gsum = g8[0]
    for q in range(1, 8):
        gsum = gsum + g8[q]
    gz[zh] = gsum
    pl.semaphore_wait(far_sem, 2)

    @pl.when(c == 1)
    def _():
        for j in Z_FAR:
            send(gz.at[zh], gz.at[zh], gz_send, gz_recv, z_of(j)[1]).start()

    arrived(r8.at[pl.ds(0, 7)], p8_send, p8_recv)
    arrived(rst.at[pl.ds(0, 7)], rst_send, rst_recv)
    psum = from_int16(r8[0], rst[0])
    for q in range(1, 8):
        psum = psum + from_int16(r8[q], rst[q])
    zb[zh], zs[zh] = to_int16(psum)
    for i, j in enumerate(Z_FAR):
        w, peer = z_of(j)
        cp = send(zb.at[zh], zb.at[zh], z_send, z_recv, peer)
        cp.start()
        cp = send(zs.at[zh], zs.at[zh], zs_send, zs_recv, peer)
        cp.start()

    other = (s + 1 - 2 * c, t)

    @pl.when(c == 1)
    def _():
        arrived(gz.at[pl.ds(0, 7)], gz_send, gz_recv)
        gsum = gz[0]
        for w in range(1, 8):
            gsum = gsum + gz[w]
        gt[...] = gsum
        send(gt, gt, gt_send, gt_recv, other).start()

    @pl.when(c == 0)
    def _():
        arrived(gt, gt_send, gt_recv)

    gsum = gt[...]
    row_id = lax.broadcasted_iota(jnp.int32, (K, 128), 0)
    lane_id = lax.broadcasted_iota(jnp.int32, (K, 128), 1)
    full = jnp.concatenate(
        [gsum] + [pltpu.roll(gsum, 128 - K * b, 1) for b in range(1, 4)], axis=0
    )
    eye = jnp.where(lane_id == row_id + K, 1.0, 0.0)
    mat = jnp.where(lane_id < K, full, eye)
    for panel in range(0, K, 8):
        cols = [
            jnp.broadcast_to(mat[:, k : k + 1], (K, 128)) for k in range(panel, panel + 8)
        ]
        for j in range(8):
            k = panel + j
            ratio = jnp.where(row_id > k, cols[j] * (1.0 / cols[j][k : k + 1, :]), 0.0)
            for l in range(j + 1, 8):
                cols[l] = cols[l] - ratio * cols[l][k : k + 1, :]
            mat = mat - ratio * mat[k : k + 1, :]
    diag = jnp.sum(jnp.where(lane_id == row_id, mat, 0.0), axis=1, keepdims=True)
    mat = mat * lax.rsqrt(diag)
    inverse = pltpu.roll(mat, 128 - K, 1)[:, :K]

    arrived(zb.at[pl.ds(0, 7)], z_send, z_recv)
    arrived(zs.at[pl.ds(0, 7)], zs_send, zs_recv)
    psum = from_int16(zb[0], zs[0])
    for w in range(1, 8):
        psum = psum + from_int16(zb[w], zs[w])
    cb[m] = jnp.dot(
        inverse, psum, preferred_element_type=jnp.float32, precision=lax.Precision.HIGHEST
    ).astype(jnp.bfloat16)
    for i, f in enumerate(OCT_FAR):
        q, peer = oct_of(f)
        cp = send(cb.at[m], cb.at[m], c8_send, c8_recv, peer)
        cp.start()

    arrived(cb.at[pl.ds(0, 7)], c8_send, c8_recv)
    for q in range(8):
        coef[:, 128 * q : 128 * q + 128] = cb[q].astype(jnp.float32)
    left(rs, rs_send, rs_recv)
    left(sk.at[:, pl.ds(0, 7 * rows)], ag_send, ag_recv.at[0])
    for blocks, send_sem, recv_sem in (
        (g8, g8_send, g8_recv), (pp, p8_send, p8_recv), (rst, rst_send, rst_recv),
        (zb, z_send, z_recv), (zs, zs_send, zs_recv), (cb, c8_send, c8_recv),
    ):
        left(blocks.at[pl.ds(0, 7)], send_sem, recv_sem)

    @pl.when(c == 1)
    def _():
        left(gz.at[pl.ds(0, 7)], gz_send, gz_recv)
        left(gt, gt_send, gt_recv)


def store(sk, coef, sketch_out, coef_out, sem):
    copies = [
        pltpu.make_async_copy(sk, sketch_out, sem.at[0]),
        pltpu.make_async_copy(coef, coef_out, sem.at[1]),
    ]
    for cp in copies:
        cp.start()
    for cp in copies:
        cp.wait()


def per_device(snapshots, omega):
    rows = snapshots.shape[0] // 8
    cols = snapshots.shape[1]
    f32, bf16 = jnp.float32, jnp.bfloat16
    dma, regular = pltpu.SemaphoreType.DMA, pltpu.SemaphoreType.REGULAR
    whole = pl.BlockSpec(memory_space=pltpu.VMEM)
    sk, coef = pl.pallas_call(
        kernel,
        name="pod",
        out_shape=(
            pltpu.VMEM((K, snapshots.shape[0]), bf16),
            pltpu.VMEM((K, cols), f32),
        ),
        in_specs=[pl.BlockSpec(memory_space=pltpu.HBM)] * 2,
        out_specs=(whole, whole),
        scratch_shapes=[
            pltpu.VMEM((8, rows, cols), bf16),
            pltpu.VMEM((K, cols), jnp.int32),
            pltpu.VMEM((8, K, rows), f32),
            pltpu.VMEM((7, K, rows), f32),
            pltpu.VMEM((8, K, 128), jnp.int16),
            pltpu.VMEM((8, K, 128), jnp.int16),
            pltpu.VMEM((8, 1, 128), f32),
            pltpu.VMEM((8, K, 128), jnp.int16),
            pltpu.VMEM((8, 1, 128), f32),
            pltpu.VMEM((8, K, 128), bf16),
            pltpu.VMEM((8, 8, 128), f32),
            pltpu.VMEM((8, 8, 128), f32),
            pltpu.VMEM((8, 128), f32),
            dma((2,)), dma, regular, regular,
        ]
        + [dma, dma, dma, dma((8,))]
        + [dma] * 16,
        compiler_params=pltpu.CompilerParams(
            collective_id=0, has_side_effects=True, vmem_limit_bytes=48 * 2**20
        ),
    )(
        pltpu.with_memory_space_constraint(snapshots, pltpu.HBM),
        pltpu.with_memory_space_constraint(omega, pltpu.HBM),
    )
    return pl.pallas_call(
        store,
        name="store",
        out_shape=(
            jax.ShapeDtypeStruct(sk.shape, sk.dtype),
            jax.ShapeDtypeStruct(coef.shape, coef.dtype),
        ),
        in_specs=[whole] * 2,
        out_specs=(pl.BlockSpec(memory_space=pl.ANY),) * 2,
        scratch_shapes=[dma((2,))],
        compiler_params=pltpu.CompilerParams(vmem_limit_bytes=4 * 2**20),
    )(sk, coef)

def solution(mesh):
    return jax.shard_map(
        per_device,
        mesh=mesh,
        in_specs=(P("space", "tm"), P(None, "tm")),
        out_specs=(P(None, "space"), P(None, "tm")),
        check_vma=False,
    )
```

```python
import jax
import jax.numpy as jnp
from jax import lax
from jax.experimental import pallas as pl
from jax.experimental.pallas import tpu as pltpu
from jax.sharding import PartitionSpec as P

MESH = pl.DeviceIdType.MESH
SNAP = 8192
K = 32
TM_FAR = ((1, 2), (1, 1), (1, 3), (1, 0), (0, 2), (0, 1), (0, 3))
OCT_FAR = ((1, 1, 0), (1, 1, 1), (1, 0, 0), (1, 0, 1), (0, 1, 0), (0, 1, 1), (0, 0, 1))
Z_FAR = (4, 3, 5, 2, 6, 1, 7)


def flip(bit, f):
    return (bit + f) % 2


def to_int16(x):
    top = jnp.max(jnp.max(jnp.abs(x), axis=0, keepdims=True), axis=1, keepdims=True)
    top = jnp.where(top > 0.0, top, 1.0)
    units = jnp.round(x * (32766.0 / top)).astype(jnp.int32).astype(jnp.int16)
    return units, jnp.broadcast_to(top * (1.0 / 32766.0), (1, 128))


def from_int16(units, step):
    return units.astype(jnp.int32).astype(jnp.float32) * step


def kernel(
    snap, omega, sk, coef,
    a, om, part, rs, pp, r8, rst, zb, zs, cb, g8, gz, gt,
    in_sem, om_sem, near_sem, far_sem,
    rs_send, rs_recv, ag_send, ag_recv, p8_send, p8_recv, z_send, z_recv,
    c8_send, c8_recv, g8_send, g8_recv, gz_send, gz_recv, zs_send, zs_recv, rst_send, rst_recv, gt_send, gt_recv,
):
    s, t = lax.axis_index("space"), lax.axis_index("tm")
    z, xl, c = s // 4, (s // 2) % 2, s % 2
    xh, y = t // 4, t % 4
    zh, zp = z // 2, z % 2
    m = zp * 4 + xl * 2 + c
    rows = a.shape[1]

    def tm_of(off):
        return flip(xh, off[0]) * 4 + (y + off[1]) % 4

    def oct_of(f):
        q = flip(zp, f[0]) * 4 + flip(xl, f[1]) * 2 + flip(c, f[2])
        return q, (zh * 8 + q, t)

    def z_of(j):
        w = (zh + j) % 8
        return w, (w * 8 + m, t)

    om_copy = pltpu.make_async_copy(omega, om, om_sem)
    om_copy.start()
    barrier = pltpu.get_barrier_semaphore()
    peers = [(s, tm_of(off)) for off in TM_FAR]
    peers += [oct_of(f)[1] for f in OCT_FAR] + [z_of(j)[1] for j in (1, 7)]
    for peer in peers:
        pl.semaphore_signal(barrier, inc=1, device_id=peer, device_id_type=MESH)

    order = [tm_of(off) for off in TM_FAR] + [t]
    loads = [
        pltpu.make_async_copy(
            snap.at[pl.ds(pl.multiple_of(d * rows, rows), rows), :], a.at[d], in_sem.at[i // 4]
        )
        for i, d in enumerate(order)
    ]
    for cp in loads[:4]:
        cp.start()

    def tell(sem, steps):
        for j in steps:
            pl.semaphore_signal(sem, inc=1, device_id=z_of(j)[1], device_id_type=MESH)

    def rows_of(d):
        return sk.at[:, pl.ds(pl.multiple_of(d * rows, rows), rows)]

    def send(src, dst, send_sem, recv_sem, peer):
        return pltpu.make_async_remote_copy(
            src_ref=src, dst_ref=dst, send_sem=send_sem, recv_sem=recv_sem,
            device_id=peer, device_id_type=MESH,
        )

    def arrived(blocks, send_sem, recv_sem):
        send(blocks, blocks, send_sem, recv_sem, peers[0]).wait_recv()

    def left(blocks, send_sem, recv_sem):
        send(blocks, blocks, send_sem, recv_sem, peers[0]).wait_send()

    om_copy.wait()
    for cp in loads[4:]:
        cp.start()
    signs = om[...].astype(jnp.float32).astype(jnp.bfloat16)
    for first in (0, 4):
        four = a.at[pl.ds(0, 4)]
        pltpu.make_async_copy(four, four, in_sem.at[first // 4]).wait()
        for i in range(first, first + 4):
            part[i] = lax.dot_general(
                signs, a[order[i]], (((1,), (1,)), ((), ())), preferred_element_type=jnp.float32
            )
        if first == 0:
            pl.semaphore_wait(barrier, len(peers))
            tell(near_sem, (1, 7))
        for i in range(first, min(first + 4, 7)):
            cp = send(part.at[i], rs.at[i], rs_send, rs_recv, (s, order[i]))
            cp.start()
    pl.semaphore_wait(near_sem, 2)
    tell(far_sem, (2, 6))

    total = part[7]
    arrived(rs, rs_send, rs_recv)
    for i in range(7):
        total = total + rs[i]
    factor = SNAP ** (-0.5)
    sk[:, pl.ds(pl.multiple_of(t * rows, rows), rows)] = (total * factor).astype(jnp.bfloat16)
    for i in range(7):
        peer = order[i] + c * (order[(i + 4) % 7] - order[i])
        cp = send(rows_of(t), rows_of(t), ag_send, ag_recv.at[t], (s, peer))
        cp.start()

    proj = None
    gram = None
    for i in (7, 5, 6, 4, 3, 1, 2, 0):
        d = order[i]
        if i < 7:
            send(rows_of(d), rows_of(d), ag_send, ag_recv.at[d], (s, d)).wait_recv()
        block = sk[:, pl.ds(pl.multiple_of(d * rows, rows), rows)]
        wide = jnp.concatenate([block] * 4, axis=0)
        g = lax.dot_general(
            block, wide, (((1,), (1,)), ((), ())), preferred_element_type=jnp.float32
        )
        p = jnp.dot(block, a[d], preferred_element_type=jnp.float32)
        gram = g if gram is None else gram + g
        proj = p if proj is None else proj + p

    lane8 = lax.broadcasted_iota(jnp.int32, (8, 128), 1) // K
    packed = jnp.zeros((8, 128), jnp.float32)
    for b in range(4):
        packed = jnp.where(lane8 == b, gram[8 * b : 8 * b + 8], packed)
    g8[m] = packed
    for i, f in enumerate(OCT_FAR):
        q, peer = oct_of(f)
        cp = send(g8.at[m], g8.at[m], g8_send, g8_recv, peer)
        cp.start()
    units, rst[m] = to_int16(proj)
    for q in range(8):
        pp[q] = units[:, 128 * q : 128 * q + 128]
    r8[m] = pp[m]
    for i, f in enumerate(OCT_FAR):
        q, peer = oct_of(f)
        cp = send(pp.at[q], r8.at[m], p8_send, p8_recv, peer)
        cp.start()
        cp = send(rst.at[m], rst.at[m], rst_send, rst_recv, peer)
        cp.start()

    arrived(g8.at[pl.ds(0, 7)], g8_send, g8_recv)
    gsum = g8[0]
    for q in range(1, 8):
        gsum = gsum + g8[q]
    gz[zh] = gsum
    pl.semaphore_wait(far_sem, 2)

    @pl.when(c == 1)
    def _():
        for j in Z_FAR:
            send(gz.at[zh], gz.at[zh], gz_send, gz_recv, z_of(j)[1]).start()

    arrived(r8.at[pl.ds(0, 7)], p8_send, p8_recv)
    arrived(rst.at[pl.ds(0, 7)], rst_send, rst_recv)
    psum = from_int16(r8[0], rst[0])
    for q in range(1, 8):
        psum = psum + from_int16(r8[q], rst[q])
    zb[zh], zs[zh] = to_int16(psum)
    for far, near in zip(Z_FAR, Z_FAR[::-1]):
        w, peer = z_of(far + c * (near - far))
        cp = send(zb.at[zh], zb.at[zh], z_send, z_recv, peer)
        cp.start()
        cp = send(zs.at[zh], zs.at[zh], zs_send, zs_recv, peer)
        cp.start()

    other = (s + 1 - 2 * c, t)

    @pl.when(c == 1)
    def _():
        arrived(gz.at[pl.ds(0, 7)], gz_send, gz_recv)
        gsum = gz[0]
        for w in range(1, 8):
            gsum = gsum + gz[w]
        gt[...] = gsum
        send(gt, gt, gt_send, gt_recv, other).start()

    @pl.when(c == 0)
    def _():
        arrived(gt, gt_send, gt_recv)

    gsum = gt[...]
    row_id = lax.broadcasted_iota(jnp.int32, (K, 128), 0)
    lane_id = lax.broadcasted_iota(jnp.int32, (K, 128), 1)
    full = jnp.concatenate(
        [gsum] + [pltpu.roll(gsum, 128 - K * b, 1) for b in range(1, 4)], axis=0
    )
    eye = jnp.where(lane_id == row_id + K, 1.0, 0.0)
    mat = jnp.where(lane_id < K, full, eye)
    for panel in range(0, K, 8):
        cols = [
            jnp.broadcast_to(mat[:, k : k + 1], (K, 128)) for k in range(panel, panel + 8)
        ]
        for j in range(8):
            k = panel + j
            ratio = jnp.where(row_id > k, cols[j] * (1.0 / cols[j][k : k + 1, :]), 0.0)
            for l in range(j + 1, 8):
                cols[l] = cols[l] - ratio * cols[l][k : k + 1, :]
            mat = mat - ratio * mat[k : k + 1, :]
    diag = jnp.sum(jnp.where(lane_id == row_id, mat, 0.0), axis=1, keepdims=True)
    mat = mat * lax.rsqrt(diag)
    inverse = pltpu.roll(mat, 128 - K, 1)[:, :K]

    arrived(zb.at[pl.ds(0, 7)], z_send, z_recv)
    arrived(zs.at[pl.ds(0, 7)], zs_send, zs_recv)
    psum = from_int16(zb[0], zs[0])
    for w in range(1, 8):
        psum = psum + from_int16(zb[w], zs[w])
    cb[m] = jnp.dot(
        inverse, psum, preferred_element_type=jnp.float32, precision=lax.Precision.HIGHEST
    ).astype(jnp.bfloat16)
    for i, f in enumerate(OCT_FAR):
        q, peer = oct_of(f)
        cp = send(cb.at[m], cb.at[m], c8_send, c8_recv, peer)
        cp.start()

    arrived(cb.at[pl.ds(0, 7)], c8_send, c8_recv)
    for q in range(8):
        coef[:, 128 * q : 128 * q + 128] = cb[q].astype(jnp.float32)
    left(rs, rs_send, rs_recv)
    left(sk.at[:, pl.ds(0, 7 * rows)], ag_send, ag_recv.at[0])
    for blocks, send_sem, recv_sem in (
        (g8, g8_send, g8_recv), (pp, p8_send, p8_recv), (rst, rst_send, rst_recv),
        (zb, z_send, z_recv), (zs, zs_send, zs_recv), (cb, c8_send, c8_recv),
    ):
        left(blocks.at[pl.ds(0, 7)], send_sem, recv_sem)

    @pl.when(c == 1)
    def _():
        left(gz.at[pl.ds(0, 7)], gz_send, gz_recv)
        left(gt, gt_send, gt_recv)


def store(sk, coef, sketch_out, coef_out, sem):
    copies = [
        pltpu.make_async_copy(sk, sketch_out, sem.at[0]),
        pltpu.make_async_copy(coef, coef_out, sem.at[1]),
    ]
    for cp in copies:
        cp.start()
    for cp in copies:
        cp.wait()


def per_device(snapshots, omega):
    rows = snapshots.shape[0] // 8
    cols = snapshots.shape[1]
    f32, bf16 = jnp.float32, jnp.bfloat16
    dma, regular = pltpu.SemaphoreType.DMA, pltpu.SemaphoreType.REGULAR
    whole = pl.BlockSpec(memory_space=pltpu.VMEM)
    sk, coef = pl.pallas_call(
        kernel,
        name="pod",
        out_shape=(
            pltpu.VMEM((K, snapshots.shape[0]), bf16),
            pltpu.VMEM((K, cols), f32),
        ),
        in_specs=[pl.BlockSpec(memory_space=pltpu.HBM)] * 2,
        out_specs=(whole, whole),
        scratch_shapes=[
            pltpu.VMEM((8, rows, cols), bf16),
            pltpu.VMEM((K, cols), jnp.int32),
            pltpu.VMEM((8, K, rows), f32),
            pltpu.VMEM((7, K, rows), f32),
            pltpu.VMEM((8, K, 128), jnp.int16),
            pltpu.VMEM((8, K, 128), jnp.int16),
            pltpu.VMEM((8, 1, 128), f32),
            pltpu.VMEM((8, K, 128), jnp.int16),
            pltpu.VMEM((8, 1, 128), f32),
            pltpu.VMEM((8, K, 128), bf16),
            pltpu.VMEM((8, 8, 128), f32),
            pltpu.VMEM((8, 8, 128), f32),
            pltpu.VMEM((8, 128), f32),
            dma((2,)), dma, regular, regular,
        ]
        + [dma, dma, dma, dma((8,))]
        + [dma] * 16,
        compiler_params=pltpu.CompilerParams(
            collective_id=0, has_side_effects=True, vmem_limit_bytes=48 * 2**20
        ),
    )(
        pltpu.with_memory_space_constraint(snapshots, pltpu.HBM),
        pltpu.with_memory_space_constraint(omega, pltpu.HBM),
    )
    return pl.pallas_call(
        store,
        name="store",
        out_shape=(
            jax.ShapeDtypeStruct(sk.shape, sk.dtype),
            jax.ShapeDtypeStruct(coef.shape, coef.dtype),
        ),
        in_specs=[whole] * 2,
        out_specs=(pl.BlockSpec(memory_space=pl.ANY),) * 2,
        scratch_shapes=[dma((2,))],
        compiler_params=pltpu.CompilerParams(vmem_limit_bytes=4 * 2**20),
    )(sk, coef)

def solution(mesh):
    return jax.shard_map(
        per_device,
        mesh=mesh,
        in_specs=(P("space", "tm"), P(None, "tm")),
        out_specs=(P(None, "space"), P(None, "tm")),
        check_vma=False,
    )
```

```python
import jax
import jax.numpy as jnp
from jax import lax
from jax.experimental import pallas as pl
from jax.experimental.pallas import tpu as pltpu
from jax.sharding import PartitionSpec as P

MESH = pl.DeviceIdType.MESH
SNAP = 8192
K = 32
TM_FAR = ((1, 2), (1, 1), (1, 3), (1, 0), (0, 2), (0, 1), (0, 3))
OCT_FAR = ((1, 1, 0), (1, 1, 1), (1, 0, 0), (1, 0, 1), (0, 1, 0), (0, 1, 1), (0, 0, 1))
Z_FAR = (4, 3, 5, 2, 6, 1, 7)


def flip(bit, f):
    return (bit + f) % 2


def to_int16(x):
    top = jnp.max(jnp.max(jnp.abs(x), axis=0, keepdims=True), axis=1, keepdims=True)
    top = jnp.where(top > 0.0, top, 1.0)
    units = jnp.round(x * (32766.0 / top)).astype(jnp.int32).astype(jnp.int16)
    return units, jnp.broadcast_to(top * (1.0 / 32766.0), (1, 128))


def from_int16(units, step):
    return units.astype(jnp.int32).astype(jnp.float32) * step


def kernel(
    snap, omega, sk, coef,
    a, om, part, rs, pp, r8, rst, zb, zs, cb, g8, gz, gt,
    in_sem, om_sem, near_sem, far_sem,
    rs_send, rs_recv, ag_send, ag_recv, p8_send, p8_recv, z_send, z_recv,
    c8_send, c8_recv, g8_send, g8_recv, gz_send, gz_recv, zs_send, zs_recv, rst_send, rst_recv, gt_send, gt_recv,
):
    s, t = lax.axis_index("space"), lax.axis_index("tm")
    z, xl, c = s // 4, (s // 2) % 2, s % 2
    xh, y = t // 4, t % 4
    zh, zp = z // 2, z % 2
    m = zp * 4 + xl * 2 + c
    rows = a.shape[1]

    def tm_of(off):
        return flip(xh, off[0]) * 4 + (y + off[1]) % 4

    def oct_of(f):
        q = flip(zp, f[0]) * 4 + flip(xl, f[1]) * 2 + flip(c, f[2])
        return q, (zh * 8 + q, t)

    def z_of(j):
        w = (zh + j) % 8
        return w, (w * 8 + m, t)

    om_copy = pltpu.make_async_copy(omega, om, om_sem)
    om_copy.start()
    barrier = pltpu.get_barrier_semaphore()
    peers = [(s, tm_of(off)) for off in TM_FAR]
    peers += [oct_of(f)[1] for f in OCT_FAR] + [z_of(j)[1] for j in (1, 7)]
    for peer in peers:
        pl.semaphore_signal(barrier, inc=1, device_id=peer, device_id_type=MESH)

    order = [tm_of(off) for off in TM_FAR] + [t]
    loads = [
        pltpu.make_async_copy(
            snap.at[pl.ds(pl.multiple_of(d * rows, rows), rows), :], a.at[d], in_sem.at[i // 4]
        )
        for i, d in enumerate(order)
    ]
    for cp in loads[:4]:
        cp.start()

    def tell(sem, steps):
        for j in steps:
            pl.semaphore_signal(sem, inc=1, device_id=z_of(j)[1], device_id_type=MESH)

    def rows_of(d):
        return sk.at[:, pl.ds(pl.multiple_of(d * rows, rows), rows)]

    def send(src, dst, send_sem, recv_sem, peer):
        return pltpu.make_async_remote_copy(
            src_ref=src, dst_ref=dst, send_sem=send_sem, recv_sem=recv_sem,
            device_id=peer, device_id_type=MESH,
        )

    def arrived(blocks, send_sem, recv_sem):
        send(blocks, blocks, send_sem, recv_sem, peers[0]).wait_recv()

    def left(blocks, send_sem, recv_sem):
        send(blocks, blocks, send_sem, recv_sem, peers[0]).wait_send()

    om_copy.wait()
    for cp in loads[4:]:
        cp.start()
    signs = om[...].astype(jnp.float32).astype(jnp.bfloat16)
    for first in (0, 4):
        four = a.at[pl.ds(0, 4)]
        pltpu.make_async_copy(four, four, in_sem.at[first // 4]).wait()
        for i in range(first, first + 4):
            part[i] = lax.dot_general(
                signs, a[order[i]], (((1,), (1,)), ((), ())), preferred_element_type=jnp.float32
            )
        if first == 0:
            pl.semaphore_wait(barrier, len(peers))
            tell(near_sem, (1, 7))
        for i in range(first, min(first + 4, 7)):
            cp = send(part.at[i], rs.at[i], rs_send, rs_recv, (s, order[i]))
            cp.start()
    pl.semaphore_wait(near_sem, 2)
    tell(far_sem, (2, 6))

    total = part[7]
    arrived(rs, rs_send, rs_recv)
    for i in range(7):
        total = total + rs[i]
    factor = SNAP ** (-0.5)
    sk[:, pl.ds(pl.multiple_of(t * rows, rows), rows)] = (total * factor).astype(jnp.bfloat16)
    for i in range(7):
        peer = order[i] + c * (order[(i + 4) % 7] - order[i])
        cp = send(rows_of(t), rows_of(t), ag_send, ag_recv.at[t], (s, peer))
        cp.start()

    proj = None
    gram = None
    for i in (7, 5, 6, 4, 3, 1, 2, 0):
        d = order[i]
        if i < 7:
            send(rows_of(d), rows_of(d), ag_send, ag_recv.at[d], (s, d)).wait_recv()
        block = sk[:, pl.ds(pl.multiple_of(d * rows, rows), rows)]
        wide = jnp.concatenate([block] * 4, axis=0)
        g = lax.dot_general(
            block, wide, (((1,), (1,)), ((), ())), preferred_element_type=jnp.float32
        )
        p = jnp.dot(block, a[d], preferred_element_type=jnp.float32)
        gram = g if gram is None else gram + g
        proj = p if proj is None else proj + p

    lane8 = lax.broadcasted_iota(jnp.int32, (8, 128), 1) // K
    packed = jnp.zeros((8, 128), jnp.float32)
    for b in range(4):
        packed = jnp.where(lane8 == b, gram[8 * b : 8 * b + 8], packed)
    g8[m] = packed
    for i, f in enumerate(OCT_FAR):
        q, peer = oct_of(f)
        cp = send(g8.at[m], g8.at[m], g8_send, g8_recv, peer)
        cp.start()
    units, rst[m] = to_int16(proj)
    for q in range(8):
        pp[q] = units[:, 128 * q : 128 * q + 128]
    r8[m] = pp[m]
    for i, f in enumerate(OCT_FAR):
        q, peer = oct_of(f)
        cp = send(pp.at[q], r8.at[m], p8_send, p8_recv, peer)
        cp.start()
        cp = send(rst.at[m], rst.at[m], rst_send, rst_recv, peer)
        cp.start()

    arrived(g8.at[pl.ds(0, 7)], g8_send, g8_recv)
    gsum = g8[0]
    for q in range(1, 8):
        gsum = gsum + g8[q]
    gz[zh] = gsum
    pl.semaphore_wait(far_sem, 2)

    @pl.when(c == 1)
    def _():
        for j in Z_FAR:
            send(gz.at[zh], gz.at[zh], gz_send, gz_recv, z_of(j)[1]).start()

    arrived(r8.at[pl.ds(0, 7)], p8_send, p8_recv)
    arrived(rst.at[pl.ds(0, 7)], rst_send, rst_recv)
    psum = from_int16(r8[0], rst[0])
    for q in range(1, 8):
        psum = psum + from_int16(r8[q], rst[q])
    zb[zh], zs[zh] = to_int16(psum)
    for far, near in zip(Z_FAR, Z_FAR[::-1]):
        w, peer = z_of(far + c * (near - far))
        cp = send(zb.at[zh], zb.at[zh], z_send, z_recv, peer)
        cp.start()
        cp = send(zs.at[zh], zs.at[zh], zs_send, zs_recv, peer)
        cp.start()

    other = (s + 1 - 2 * c, t)

    @pl.when(c == 1)
    def _():
        arrived(gz.at[pl.ds(0, 7)], gz_send, gz_recv)
        gsum = gz[0]
        for w in range(1, 8):
            gsum = gsum + gz[w]
        gt[...] = gsum
        send(gt, gt, gt_send, gt_recv, other).start()

    @pl.when(c == 0)
    def _():
        arrived(gt, gt_send, gt_recv)

    gsum = gt[...]
    row_id = lax.broadcasted_iota(jnp.int32, (K, 128), 0)
    lane_id = lax.broadcasted_iota(jnp.int32, (K, 128), 1)
    full = jnp.concatenate(
        [gsum] + [pltpu.roll(gsum, 128 - K * b, 1) for b in range(1, 4)], axis=0
    )
    eye = jnp.where(lane_id == row_id + K, 1.0, 0.0)
    mat = jnp.where(lane_id < K, full, eye)
    for panel in range(0, K, 8):
        cols = [
            jnp.broadcast_to(mat[:, k : k + 1], (K, 128)) for k in range(panel, panel + 8)
        ]
        for j in range(8):
            k = panel + j
            ratio = jnp.where(row_id > k, cols[j] * (1.0 / cols[j][k : k + 1, :]), 0.0)
            for l in range(j + 1, 8):
                cols[l] = cols[l] - ratio * cols[l][k : k + 1, :]
            mat = mat - ratio * mat[k : k + 1, :]
    diag = jnp.sum(jnp.where(lane_id == row_id, mat, 0.0), axis=1, keepdims=True)
    mat = mat * lax.rsqrt(diag)
    inverse = pltpu.roll(mat, 128 - K, 1)[:, :K]

    arrived(zb.at[pl.ds(0, 7)], z_send, z_recv)
    arrived(zs.at[pl.ds(0, 7)], zs_send, zs_recv)
    psum = from_int16(zb[0], zs[0])
    for w in range(1, 8):
        psum = psum + from_int16(zb[w], zs[w])
    cb[m] = jnp.dot(
        inverse, psum, preferred_element_type=jnp.float32, precision=lax.Precision.HIGHEST
    ).astype(jnp.bfloat16)
    for i, f in enumerate(OCT_FAR):
        (_, (sq, _)), (_, (su, _)) = oct_of(f), oct_of(OCT_FAR[6 - i])
        peer = (su + c * (sq - su), t)
        cp = send(cb.at[m], cb.at[m], c8_send, c8_recv, peer)
        cp.start()

    arrived(cb.at[pl.ds(0, 7)], c8_send, c8_recv)
    for q in range(8):
        coef[:, 128 * q : 128 * q + 128] = cb[q].astype(jnp.float32)
    left(rs, rs_send, rs_recv)
    left(sk.at[:, pl.ds(0, 7 * rows)], ag_send, ag_recv.at[0])
    for blocks, send_sem, recv_sem in (
        (g8, g8_send, g8_recv), (pp, p8_send, p8_recv), (rst, rst_send, rst_recv),
        (zb, z_send, z_recv), (zs, zs_send, zs_recv), (cb, c8_send, c8_recv),
    ):
        left(blocks.at[pl.ds(0, 7)], send_sem, recv_sem)

    @pl.when(c == 1)
    def _():
        left(gz.at[pl.ds(0, 7)], gz_send, gz_recv)
        left(gt, gt_send, gt_recv)


def store(sk, coef, sketch_out, coef_out, sem):
    copies = [
        pltpu.make_async_copy(sk, sketch_out, sem.at[0]),
        pltpu.make_async_copy(coef, coef_out, sem.at[1]),
    ]
    for cp in copies:
        cp.start()
    for cp in copies:
        cp.wait()


def per_device(snapshots, omega):
    rows = snapshots.shape[0] // 8
    cols = snapshots.shape[1]
    f32, bf16 = jnp.float32, jnp.bfloat16
    dma, regular = pltpu.SemaphoreType.DMA, pltpu.SemaphoreType.REGULAR
    whole = pl.BlockSpec(memory_space=pltpu.VMEM)
    sk, coef = pl.pallas_call(
        kernel,
        name="pod",
        out_shape=(
            pltpu.VMEM((K, snapshots.shape[0]), bf16),
            pltpu.VMEM((K, cols), f32),
        ),
        in_specs=[pl.BlockSpec(memory_space=pltpu.HBM)] * 2,
        out_specs=(whole, whole),
        scratch_shapes=[
            pltpu.VMEM((8, rows, cols), bf16),
            pltpu.VMEM((K, cols), jnp.int32),
            pltpu.VMEM((8, K, rows), f32),
            pltpu.VMEM((7, K, rows), f32),
            pltpu.VMEM((8, K, 128), jnp.int16),
            pltpu.VMEM((8, K, 128), jnp.int16),
            pltpu.VMEM((8, 1, 128), f32),
            pltpu.VMEM((8, K, 128), jnp.int16),
            pltpu.VMEM((8, 1, 128), f32),
            pltpu.VMEM((8, K, 128), bf16),
            pltpu.VMEM((8, 8, 128), f32),
            pltpu.VMEM((8, 8, 128), f32),
            pltpu.VMEM((8, 128), f32),
            dma((2,)), dma, regular, regular,
        ]
        + [dma, dma, dma, dma((8,))]
        + [dma] * 16,
        compiler_params=pltpu.CompilerParams(
            collective_id=0, has_side_effects=True, vmem_limit_bytes=48 * 2**20
        ),
    )(
        pltpu.with_memory_space_constraint(snapshots, pltpu.HBM),
        pltpu.with_memory_space_constraint(omega, pltpu.HBM),
    )
    return pl.pallas_call(
        store,
        name="store",
        out_shape=(
            jax.ShapeDtypeStruct(sk.shape, sk.dtype),
            jax.ShapeDtypeStruct(coef.shape, coef.dtype),
        ),
        in_specs=[whole] * 2,
        out_specs=(pl.BlockSpec(memory_space=pl.ANY),) * 2,
        scratch_shapes=[dma((2,))],
        compiler_params=pltpu.CompilerParams(vmem_limit_bytes=4 * 2**20),
    )(sk, coef)

def solution(mesh):
    return jax.shard_map(
        per_device,
        mesh=mesh,
        in_specs=(P("space", "tm"), P(None, "tm")),
        out_specs=(P(None, "space"), P(None, "tm")),
        check_vma=False,
    )
```
